256 devices in a mesh: src: 16 (over y, x), tgt: 16 (over z, core).
Axes of the slice: x: 4, y: 4, z: 8, core: 2. Of those that a mesh axis runs over, the one named last changes fastest.
Arguments:
- tile_cost: bfloat16 [3072, 512, 512], P(('src', 'tgt')), may hold values from -2.5 to 7.5
- tile_pairs: int32 [3072, 2], P(('src', 'tgt')), may hold values from 0 to 191, as said below
- tile_counts: int32 [256], P(('src', 'tgt')), may hold values from 3 to 12, as said below
- src_mass: float32 [98304], P('src'), may hold values from 0.25 to 4
- tgt_mass: float32 [98304], P('tgt'), may hold values from 0.25 to 4
- targets_t: bfloat16 [64, 98304], P(None, 'tgt'), may hold values from -18 to 18
Outputs:
- mapped_t: float32 [64, 98304], P(None, ('src', 'tgt'))
The draws below stay inside these ranges and needn't reach their ends.
Inputs may be any that keep to these rules, and one draw needn't show every extreme that they name: `tile_pairs`: device d of the src+tgt order owns slots d * 12 to (d + 1) * 12 - 1. Its first tile_counts[d] slots hold distinct kept pairs whose source tile lies among its src index's 12 tiles and whose target tile among its tgt index's 12 tiles; its other slots repeat its first slot. Every source tile is in exactly 8 kept pairs, every target tile in at least one. `tile_counts`: over the devices of one src index the counts sum to 96; some device of every src index holds 12; every device holds at least (16 * 6 - 12) // (16 - 1) - 2.
All inputs are finite; a program needn't handle non-finite values.
Results may differ from the reference program's by a relative error of at most 0.0029.
Values may be sent and summed in bfloat16 or wider, within the bound.
No kernel may reach another device: no remote copies, remote signals or barrier semaphores. Data moves between devices by JAX's collectives and lax.ppermute only.
A program may use at most 64 MiB of HBM per device.

```python
import math
import jax
import jax.numpy as jnp
from jax import lax

TILE = 512
DIM = 64
LOAD = 6
TGT_TILES = 12
ITERS = 2
CAP = 12
SRC_TILES = 12
NS = 98304
NT = 98304
N_SRC = 16
N_TGT = 16


def tile_layout(key):
    base_key = jax.random.fold_in(key, 7)
    row_keys = jax.random.split(base_key, N_SRC)

    def one_row(row_key):
        order_key, move_key = jax.random.split(row_key)
        order = jax.random.permutation(order_key, N_TGT).astype(jnp.int32)
        remain = N_TGT * LOAD - CAP
        basic = remain // (N_TGT - 1)
        extra = remain % (N_TGT - 1)
        position = jnp.arange(N_TGT, dtype=jnp.int32)
        profile = jnp.where(position == 0, CAP, basic + (position - 1 < extra).astype(jnp.int32))
        moves = jax.random.randint(move_key, (N_TGT,), 0, 3).astype(jnp.int32)
        giving = jnp.where((position % 2 == 1) & (position + 1 < N_TGT), moves, 0)
        received = jnp.concatenate([jnp.zeros((1,), jnp.int32), giving[:-1]])
        profile = (profile - giving + received).astype(jnp.int32)
        return jnp.zeros((N_TGT,), jnp.int32).at[order].set(profile)
    counts = jax.vmap(one_row)(row_keys)
    row_start = jnp.cumsum(counts, axis=1) - counts
    col_start = jnp.cumsum(counts, axis=0) - counts
    slot_range = jnp.arange(CAP, dtype=jnp.int32)
    alive = slot_range[None, None, :] < counts[:, :, None]
    used = jnp.where(alive, slot_range[None, None, :], 0)
    src_local = (row_start[:, :, None] + used) % SRC_TILES
    tgt_local = (col_start[:, :, None] + used) % TGT_TILES
    src_block = jnp.arange(N_SRC, dtype=jnp.int32)[:, None, None] * SRC_TILES
    tgt_block = jnp.arange(N_TGT, dtype=jnp.int32)[None, :, None] * TGT_TILES
    pairs = jnp.stack([src_block + src_local, tgt_block + tgt_local], axis=-1).astype(jnp.int32)
    return (counts.reshape(-1), pairs.reshape(N_SRC * N_TGT * CAP, 2))


def draw_tile_pairs(key, part):
    return tile_layout(key)[1]


def draw_tile_counts(key, part):
    return tile_layout(key)[0]


def draw_tile_cost(key, part):
    first_key = jax.random.fold_in(jax.random.fold_in(key, 11), 0)
    shape = (N_SRC * N_TGT * CAP, TILE, TILE)
    return jax.random.uniform(first_key, shape, jnp.float32, 0.0, 4.0).astype(jnp.bfloat16)


def block_scale(key, extent, shards, smallest, high):
    def one(axis_at, shards_of):
        heights = jax.random.uniform(jax.random.fold_in(jax.random.fold_in(key, 6), axis_at), (shards_of,), jnp.float32, smallest / len(shards), high / len(shards))
        return jnp.repeat(jnp.exp(heights), extent[axis_at] // shards_of).reshape((-1,) + (1,) * (len(extent) - axis_at - 1))

    factor_of = one(*shards[0])
    for cut in shards[1:]:
        factor_of = factor_of * one(*cut)
    return factor_of


def centred(stream_key, shape, scale, most, shards=(), kind=jnp.bfloat16):
    drawn = scale * jax.random.normal(stream_key, shape, jnp.float32)
    if shards:
        drawn = drawn * block_scale(stream_key, shape, shards, -0.22, 0.18)
    return jnp.clip(drawn, -most, most).astype(kind)


def setup_inputs(seed: int = 0) -> dict:
    streams_of = jax.random.split(jax.random.key(seed), 7)
    tile_cost = draw_tile_cost(jax.random.fold_in(streams_of[6], 71), 0)
    tile_pairs = draw_tile_pairs(jax.random.fold_in(streams_of[6], 71), 0)
    tile_counts = draw_tile_counts(jax.random.fold_in(streams_of[6], 71), 0)
    src_mass = jnp.clip(jnp.exp(math.log(4.0) - 2.7725887 * jax.random.uniform(streams_of[3], (NS,), jnp.float32) ** block_scale(streams_of[3], (NS,), ((0, 16),), -0.2, 0.2)), 0.25, 4.0)
    tgt_mass = jnp.clip(jnp.exp(math.log(4.0) - 2.7725887 * jax.random.uniform(streams_of[4], (NT,), jnp.float32) ** block_scale(streams_of[4], (NT,), ((0, 16),), -0.2, 0.2)), 0.25, 4.0)
    targets_t = centred(streams_of[5], (DIM, NT), 3.0, 18.0, ((1, 16),))
    return {"tile_cost": tile_cost, "tile_pairs": tile_pairs, "tile_counts": tile_counts, "src_mass": src_mass, "tgt_mass": tgt_mass, "targets_t": targets_t}


entropic = 0.02
negative_floor = -1e30


def fold_pair(first, second):
    larger = jnp.maximum(first[0], second[0])
    return (larger, first[1] * jnp.exp(first[0] - larger) + second[1] * jnp.exp(second[0] - larger))


def merge_into(totals, position, part):
    before = (lax.dynamic_index_in_dim(totals[0], position, 0, False), lax.dynamic_index_in_dim(totals[1], position, 0, False))
    after = fold_pair(before, part)
    return (lax.dynamic_update_index_in_dim(totals[0], after[0], position, 0), lax.dynamic_update_index_in_dim(totals[1], after[1], position, 0))


def potential(merged, masses):
    return entropic * jnp.log(masses) - entropic * (merged[0] + jnp.log(merged[1])).reshape(-1)


def reference(tile_cost, tile_pairs, tile_counts, src_mass, tgt_mass, targets_t):
    slot_total = tile_cost.shape[0]
    edge = tile_cost.shape[1]
    slot_ids = jnp.arange(slot_total, dtype=jnp.int32)
    alive = (slot_ids % CAP) < jnp.repeat(tile_counts, CAP, total_repeat_length=slot_total)
    src_tiles = src_mass.shape[0] // edge
    tgt_tiles = tgt_mass.shape[0] // edge

    def empty_pair(count):
        return (jnp.full((count, edge), negative_floor, jnp.float32), jnp.zeros((count, edge), jnp.float32))

    def row_sweep(tgt_pot):
        def advance(totals, slot_index):
            cost_tile = tile_cost[slot_index].astype(jnp.float32)
            src_tile = tile_pairs[slot_index, 0].astype(jnp.int32)
            tgt_tile = tile_pairs[slot_index, 1].astype(jnp.int32)
            column_pot = lax.dynamic_slice_in_dim(tgt_pot, tgt_tile * edge, edge)
            scores = (column_pot[None, :] - cost_tile) / entropic
            maxima = jnp.max(scores, axis=1)
            sums = jnp.sum(jnp.exp(scores - maxima[:, None]), axis=1)
            maxima = jnp.where(alive[slot_index], maxima, negative_floor)
            sums = jnp.where(alive[slot_index], sums, 0.0)
            return merge_into(totals, src_tile, (maxima, sums)), None
        result, unused = lax.scan(advance, empty_pair(src_tiles), slot_ids)
        return result

    def col_sweep(src_pot):
        def advance(totals, slot_index):
            cost_tile = tile_cost[slot_index].astype(jnp.float32)
            src_tile = tile_pairs[slot_index, 0].astype(jnp.int32)
            tgt_tile = tile_pairs[slot_index, 1].astype(jnp.int32)
            row_pot = lax.dynamic_slice_in_dim(src_pot, src_tile * edge, edge)
            scores = (row_pot[:, None] - cost_tile) / entropic
            maxima = jnp.max(scores, axis=0)
            sums = jnp.sum(jnp.exp(scores - maxima[None, :]), axis=0)
            maxima = jnp.where(alive[slot_index], maxima, negative_floor)
            sums = jnp.where(alive[slot_index], sums, 0.0)
            return merge_into(totals, tgt_tile, (maxima, sums)), None
        result, unused = lax.scan(advance, empty_pair(tgt_tiles), slot_ids)
        return result

    def map_sweep(src_pot, tgt_pot):
        def advance(totals, slot_index):
            numer, denom = totals
            cost_tile = tile_cost[slot_index].astype(jnp.float32)
            src_tile = tile_pairs[slot_index, 0].astype(jnp.int32)
            tgt_tile = tile_pairs[slot_index, 1].astype(jnp.int32)
            row_pot = lax.dynamic_slice_in_dim(src_pot, src_tile * edge, edge)
            column_pot = lax.dynamic_slice_in_dim(tgt_pot, tgt_tile * edge, edge)
            weights = jnp.exp((row_pot[:, None] + column_pot[None, :] - cost_tile) / entropic)
            weights = jnp.where(alive[slot_index], weights, 0.0)
            old_mass = lax.dynamic_index_in_dim(denom, src_tile, 0, False)
            denom = lax.dynamic_update_index_in_dim(denom, old_mass + jnp.sum(weights, axis=1), src_tile, 0)
            columns = lax.dynamic_slice_in_dim(targets_t, tgt_tile * edge, edge, 1)
            part = lax.dot_general(columns, weights.astype(jnp.bfloat16), (((1,), (1,)), ((), ())), preferred_element_type=jnp.float32)
            current = lax.dynamic_slice_in_dim(numer, src_tile * edge, edge, 1)
            numer = lax.dynamic_update_slice_in_dim(numer, current + part, src_tile * edge, 1)
            return (numer, denom), None
        start = (jnp.zeros((targets_t.shape[0], src_mass.shape[0]), jnp.float32), jnp.zeros((src_tiles, edge), jnp.float32))
        result, unused = lax.scan(advance, start, slot_ids)
        return result

    tgt_pot = jnp.zeros(tgt_mass.shape, jnp.float32)
    src_pot = jnp.zeros(src_mass.shape, jnp.float32)
    for repeat_index in range(ITERS):
        src_pot = potential(row_sweep(tgt_pot), src_mass)
        tgt_pot = potential(col_sweep(src_pot), tgt_mass)
    numer, denom = map_sweep(src_pot, tgt_pot)
    return numer / denom.reshape(-1)[None, :]
```

```python
import functools
import math

import jax
import jax.numpy as jnp
from jax import lax
from jax.experimental import pallas as pl
from jax.experimental.pallas import tpu as pltpu
from jax.sharding import PartitionSpec as P

ENTROPIC = 0.02
SCALE = math.log2(math.e) / ENTROPIC
FLOOR = -1e30
BAND = 128


def start_tiles(count, costs, held, sems):
    def issue(k, carry):
        pltpu.make_async_copy(costs.at[k], held.at[k], sems.at[k]).start()
        return carry

    lax.fori_loop(0, count, issue, 0)


def wait_tile(k, costs, held, sems):
    pltpu.make_async_copy(costs.at[k], held.at[k], sems.at[k]).wait()


def log_sum(parts):
    top = functools.reduce(jnp.maximum, parts)
    total = sum(jnp.exp2(part - top) for part in parts)
    return top + jnp.log2(total)


def log_sum_refs(refs):
    return log_sum([ref[...] for ref in refs])


def lanes(k):
    return slice(k * BAND, (k + 1) * BAND)


def down(row):
    return jnp.broadcast_to(row, (BAND, BAND)).T


def across(block):
    return jnp.sum(block.T, axis=0, keepdims=True)


def spread(ref, block):
    for k in range(ref.shape[0]):
        ref[k] = block[k:k + 1]


def advance(ref, old, block):
    for k in range(ref.shape[0]):
        ref[k] = old[k] + block[k:k + 1]


def gather(ref, rows):
    for k in range(ref.shape[0]):
        ref[k:k + 1] = rows[k]


def scaled(held, k, band, strip):
    return held[k, lanes(band), lanes(strip)].astype(jnp.float32) * SCALE


def fold(block):
    return jnp.sum(block.reshape(-1, 8, BAND), axis=0)


def first_rows(edge, tiles, pairs, counts, costs, out, found, held, sems):
    count = counts[0]
    start_tiles(count, costs, held, sems)
    found[...] = jnp.full(found.shape, FLOOR, jnp.float32)
    bands = edge // BAND

    def visit(k, carry):
        wait_tile(k, costs, held, sems)
        tile = lax.rem(pairs[k, 0], tiles)
        for band in range(bands):
            blocks = [scaled(held, k, band, strip) for strip in range(bands)]
            least = jnp.min(functools.reduce(jnp.minimum, blocks), axis=1, keepdims=True)
            total = sum(jnp.exp2(least - block) for block in blocks)
            part = jnp.log2(across(total)) - jnp.broadcast_to(least, (BAND, BAND)).T[0:1]
            where = (tile, slice(None), lanes(band))
            found[where] = log_sum([found[where], part])
        return carry

    lax.fori_loop(0, count, visit, 0)
    gather(out, found)


def first_columns(edge, src_tiles, tgt_tiles, pairs, counts, costs, p0, p1, p2, p3, mass, out, rows, found, held, sems):
    count = counts[0]
    start_tiles(count, costs, held, sems)
    found[...] = jnp.full(found.shape, FLOOR, jnp.float32)
    spread(rows, jnp.log2(mass[...]) - log_sum_refs((p0, p1, p2, p3)))
    bands = edge // BAND

    def visit(k, carry):
        wait_tile(k, costs, held, sems)
        src = lax.rem(pairs[k, 0], src_tiles)
        tgt = lax.rem(pairs[k, 1], tgt_tiles)
        tops = [jnp.full((8, BAND), FLOOR, jnp.float32)] * bands
        sums = [jnp.zeros((8, BAND), jnp.float32)] * bands
        for band in range(bands):
            row_pot = down(rows[src, :, lanes(band)])
            for strip in range(bands):
                score = (row_pot - scaled(held, k, band, strip)).reshape(-1, 8, BAND)
                top = jnp.maximum(tops[strip], jnp.max(score, axis=0))
                sums[strip] = sums[strip] * jnp.exp2(tops[strip] - top) + jnp.sum(jnp.exp2(score - top[None]), axis=0)
                tops[strip] = top
        for strip in range(bands):
            top = jnp.max(tops[strip], axis=0, keepdims=True)
            total = jnp.sum(sums[strip] * jnp.exp2(tops[strip] - top), axis=0, keepdims=True)
            where = (tgt, slice(None), lanes(strip))
            found[where] = log_sum([found[where], top + jnp.log2(total)])
        return carry

    lax.fori_loop(0, count, visit, 0)
    gather(out, found)


def later_rows(edge, src_tiles, tgt_tiles, pairs, counts, costs, rows, p0, p1, p2, p3, mass, out, cols, found, held, sems):
    count = counts[0]
    start_tiles(count, costs, held, sems)
    found[...] = jnp.zeros(found.shape, jnp.float32)
    spread(cols, jnp.log2(mass[...]) - log_sum_refs((p0, p1, p2, p3)))
    bands = edge // BAND

    def visit(k, carry):
        wait_tile(k, costs, held, sems)
        src = lax.rem(pairs[k, 0], src_tiles)
        tgt = lax.rem(pairs[k, 1], tgt_tiles)
        for band in range(bands):
            row_pot = down(rows[src, :, lanes(band)])
            total = 0.0
            for strip in range(bands):
                pot = row_pot + cols[tgt, :, lanes(strip)]
                total = total + jnp.exp2(pot - scaled(held, k, band, strip))
            where = (src, slice(None), lanes(band))
            found[where] = found[where] + across(total)
        return carry

    lax.fori_loop(0, count, visit, 0)
    gather(out, found)


def later_columns(edge, src_tiles, tgt_tiles, pairs, counts, costs, rows, cols, p0, p1, p2, p3, mass, out, new_rows, found, held, sems):
    count = counts[0]
    start_tiles(count, costs, held, sems)
    found[...] = jnp.zeros(found.shape, jnp.float32)
    advance(new_rows, rows, jnp.log2(mass[...]) - jnp.log2(p0[...] + p1[...] + p2[...] + p3[...]))
    bands = edge // BAND

    def visit(k, carry):
        wait_tile(k, costs, held, sems)
        src = lax.rem(pairs[k, 0], src_tiles)
        tgt = lax.rem(pairs[k, 1], tgt_tiles)
        sums = [jnp.zeros((8, BAND), jnp.float32)] * bands
        for band in range(bands):
            row_pot = down(new_rows[src, :, lanes(band)])
            for strip in range(bands):
                pot = row_pot + cols[tgt, :, lanes(strip)]
                sums[strip] = sums[strip] + fold(jnp.exp2(pot - scaled(held, k, band, strip)))
        for strip in range(bands):
            where = (tgt, slice(None), lanes(strip))
            found[where] = found[where] + jnp.sum(sums[strip], axis=0, keepdims=True)
        return carry

    lax.fori_loop(0, count, visit, 0)
    gather(out, found)


def map_tiles(edge, src_tiles, tgt_tiles, core_axis, pairs, counts, costs, rows, cols, p0, p1, p2, p3, mass, targets,
              mine, other, new_cols, total, held, sems):
    count = counts[0]
    start_tiles(count, costs, held, sems)
    total[...] = jnp.zeros(total.shape, jnp.float32)
    advance(new_cols, cols, jnp.log2(mass[...]) - jnp.log2(p0[...] + p1[...] + p2[...] + p3[...]))
    bands = edge // BAND
    dim = targets.shape[0]

    def visit(k, carry):
        wait_tile(k, costs, held, sems)
        src = lax.rem(pairs[k, 0], src_tiles)
        tgt = lax.rem(pairs[k, 1], tgt_tiles)
        points = targets[:, pl.ds(pl.multiple_of(tgt * edge, edge), edge)]
        for pair in range(bands // 2):
            rounded = []
            sums = []
            for band in (2 * pair, 2 * pair + 1):
                row_pot = down(rows[src, :, lanes(band)])
                weights = [
                    jnp.exp2(row_pot + new_cols[tgt, :, lanes(strip)] - scaled(held, k, band, strip))
                    for strip in range(bands)
                ]
                sums.append(across(sum(weights)))
                rounded.append(jnp.concatenate([w.astype(jnp.bfloat16) for w in weights], axis=1))
            both = jnp.concatenate(rounded, axis=0)
            part = lax.dot_general(points, both, (((1,), (1,)), ((), ())), preferred_element_type=jnp.float32)
            where = pl.ds(pl.multiple_of(src * edge + pair * 2 * BAND, 2 * BAND), 2 * BAND)
            total[0:dim, where] = total[0:dim, where] + part
            total[dim:dim + 1, where] = total[dim:dim + 1, where] + jnp.concatenate(sums, axis=1)
        return carry

    lax.fori_loop(0, count, visit, 0)
    share = mine.shape[2]
    core = lax.rem(lax.axis_index(core_axis), 2)
    for z in range(mine.shape[0]):
        own = pl.ds(pl.multiple_of((2 * z + core) * share, BAND), share)
        mine[z] = total[:, own]
        far = pl.ds(pl.multiple_of((2 * z + 1 - core) * share, BAND), share)
        split_mass(other, z, total[0:dim, far], total[dim:dim + 1, far])


def split_mass(ref, z, numer, mass):
    dim = numer.shape[0]
    ref[z, 0:dim] = numer.astype(jnp.bfloat16)
    high = mass.astype(jnp.bfloat16)
    low = (mass - high.astype(jnp.float32)).astype(jnp.bfloat16)
    row = lax.broadcasted_iota(jnp.int32, (8, mass.shape[1]), 0)
    tail = jnp.where(row == 0, high.astype(jnp.float32), jnp.where(row == 1, low.astype(jnp.float32), 0.0))
    ref[z, dim:dim + 8] = tail.astype(jnp.bfloat16)


def join_pair(dim, mine, got, out):
    for z in range(mine.shape[0]):
        arrived = got[z].astype(jnp.float32)
        numer = mine[z, 0:dim] + arrived[0:dim]
        mass = mine[z, dim:dim + 1] + arrived[dim:dim + 1] + arrived[dim + 1:dim + 2]
        split_mass(out, z, numer, mass)


def finish(dim, parts, out):
    total = parts[0].astype(jnp.float32)
    for z in range(1, parts.shape[0]):
        total = total + parts[z].astype(jnp.float32)
    out[...] = total[0:dim] / (total[dim:dim + 1] + total[dim + 1:dim + 2])


def exchange(array, axis, distances):
    size = lax.axis_size(axis)
    return [lax.ppermute(array, axis, [(i, i ^ d) for i in range(size)]) for d in distances]


def quarters(array, axis, combine):
    array = combine([array, *exchange(array, axis, (1, 2, 3))])
    return [array, *exchange(array, axis, (4, 8, 12))]


def local(tile_cost, tile_pairs, tile_counts, src_mass, tgt_mass, targets_t):
    slots, edge = tile_cost.shape[0], tile_cost.shape[1]
    src_tiles = src_mass.shape[0] // edge
    tgt_tiles = tgt_mass.shape[0] // edge
    dim = targets_t.shape[0]
    group = lax.axis_size("tgt")
    src_mass = src_mass.reshape(src_tiles, edge)
    tgt_mass = tgt_mass.reshape(tgt_tiles, edge)
    smem = pl.BlockSpec(memory_space=pltpu.SMEM)
    vmem = pl.BlockSpec(memory_space=pltpu.VMEM)
    anywhere = pl.BlockSpec(memory_space=pl.ANY)
    by_src = jax.ShapeDtypeStruct((src_tiles, edge), jnp.float32)
    by_tgt = jax.ShapeDtypeStruct((tgt_tiles, edge), jnp.float32)
    src_rows = jax.ShapeDtypeStruct((src_tiles, 1, edge), jnp.float32)
    tgt_rows = jax.ShapeDtypeStruct((tgt_tiles, 1, edge), jnp.float32)
    src_found = [pltpu.VMEM(src_rows.shape, jnp.float32)]
    tgt_found = [pltpu.VMEM(tgt_rows.shape, jnp.float32)]
    tiles = (tile_pairs, tile_counts, tile_cost)
    tile_scratch = [pltpu.VMEM(tile_cost.shape, tile_cost.dtype), pltpu.SemaphoreType.DMA((slots,))]

    def over_tiles(body, outs, operands, scratch=()):
        return pl.pallas_call(
            body,
            out_shape=outs,
            in_specs=[smem, smem, anywhere] + [vmem] * len(operands),
            out_specs=jax.tree.map(lambda _: vmem, outs),
            scratch_shapes=[*scratch, *tile_scratch],
        )(*tiles, *operands)

    sizes = (edge, src_tiles, tgt_tiles)
    row_part = over_tiles(functools.partial(first_rows, edge, src_tiles), by_src, (), src_found)
    row_parts = quarters(row_part, "tgt", log_sum)
    col_part, rows = over_tiles(functools.partial(first_columns, *sizes), (by_tgt, src_rows), (*row_parts, src_mass), tgt_found)
    col_parts = quarters(col_part, "src", log_sum)
    row_part, cols = over_tiles(functools.partial(later_rows, *sizes), (by_src, tgt_rows), (rows, *col_parts, tgt_mass), src_found)
    row_parts = quarters(row_part, "tgt", sum)
    col_part, rows = over_tiles(
        functools.partial(later_columns, *sizes), (by_tgt, src_rows), (rows, cols, *row_parts, src_mass), tgt_found
    )
    col_parts = quarters(col_part, "src", sum)
    share = src_mass.size // group
    half = group // 2
    wire = jax.ShapeDtypeStruct((half, dim + 8, share), jnp.bfloat16)
    mine, other = over_tiles(
        functools.partial(map_tiles, *sizes, "tgt"),
        (jax.ShapeDtypeStruct((half, dim + 8, share), jnp.float32), wire),
        (rows, cols, *col_parts, tgt_mass, targets_t),
        [*tgt_found, pltpu.VMEM((dim + 8, src_mass.size), jnp.float32)],
    )
    (got,) = exchange(other, "tgt", (1,))
    joined = pl.pallas_call(
        functools.partial(join_pair, dim), out_shape=wire, in_specs=[vmem] * 2, out_specs=vmem
    )(mine, got)
    parts = lax.all_to_all(
        joined, "tgt", 0, 0, axis_index_groups=[[2 * z + c for z in range(half)] for c in range(2)]
    )
    return pl.pallas_call(
        functools.partial(finish, dim),
        out_shape=jax.ShapeDtypeStruct((dim, share), jnp.float32),
        in_specs=[vmem],
        out_specs=vmem,
    )(parts)


def solution(mesh):
    return jax.shard_map(
        local,
        mesh=mesh,
        in_specs=(
            P(("src", "tgt"), None, None),
            P(("src", "tgt"), None),
            P(("src", "tgt")),
            P("src"),
            P("tgt"),
            P(None, "tgt"),
        ),
        out_specs=P(None, ("src", "tgt")),
        check_vma=False,
    )
```

```python
import functools
import math

import jax
import jax.numpy as jnp
from jax import lax
from jax.experimental import pallas as pl
from jax.experimental.pallas import tpu as pltpu
from jax.sharding import PartitionSpec as P

ENTROPIC = 0.02
SCALE = math.log2(math.e) / ENTROPIC
FLOOR = -1e30
BAND = 128


def start_tiles(count, costs, held, sems):
    def issue(k, carry):
        pltpu.make_async_copy(costs.at[k], held.at[k], sems.at[k]).start()
        return carry

    lax.fori_loop(0, count, issue, 0)


def wait_tile(k, costs, held, sems):
    pltpu.make_async_copy(costs.at[k], held.at[k], sems.at[k]).wait()


def log_sum(parts):
    top = functools.reduce(jnp.maximum, parts)
    total = sum(jnp.exp2(part - top) for part in parts)
    return top + jnp.log2(total)


def log_sum_refs(refs):
    return log_sum([ref[...] for ref in refs])


def lanes(k):
    return slice(k * BAND, (k + 1) * BAND)


def down(row):
    return jnp.broadcast_to(row, (BAND, BAND)).T


def across(block):
    return jnp.sum(block.T, axis=0, keepdims=True)


def stacked(ref):
    return jnp.concatenate([ref[k] for k in range(ref.shape[0])], axis=0)


def spread(ref, block):
    for k in range(ref.shape[0]):
        ref[k] = block[k:k + 1]


def advance(ref, old, block):
    for k in range(ref.shape[0]):
        ref[k] = old[k] + block[k:k + 1]


def gather(ref, rows):
    for k in range(ref.shape[0]):
        ref[k:k + 1] = rows[k]


def scaled(held, k, band, strip):
    return held[k, lanes(band), lanes(strip)].astype(jnp.float32) * SCALE


def fold(block):
    return jnp.sum(block.reshape(-1, 8, BAND), axis=0)


def first_rows(edge, tiles, pairs, counts, costs, out, held, found, sems):
    count = counts[0]
    start_tiles(count, costs, held, sems)
    found[...] = jnp.full(found.shape, FLOOR, jnp.float32)
    bands = edge // BAND

    def visit(k, carry):
        wait_tile(k, costs, held, sems)
        tile = lax.rem(pairs[0, k], tiles)
        for band in range(bands):
            blocks = [scaled(held, k, band, strip) for strip in range(bands)]
            least = jnp.min(functools.reduce(jnp.minimum, blocks), axis=1, keepdims=True)
            total = sum(jnp.exp2(least - block) for block in blocks)
            part = jnp.log2(across(total)) - jnp.broadcast_to(least, (BAND, BAND)).T[0:1]
            where = (tile, slice(None), lanes(band))
            found[where] = log_sum([found[where], part])
        return carry

    lax.fori_loop(0, count, visit, 0)
    gather(out, found)


def first_columns(edge, src_tiles, tgt_tiles, pairs, counts, held, p0, p1, p2, p3, mass, out, rows, found):
    count = counts[0]
    found[...] = jnp.full(found.shape, FLOOR, jnp.float32)
    spread(rows, jnp.log2(stacked(mass)) - log_sum_refs((p0, p1, p2, p3)))
    bands = edge // BAND

    def visit(k, carry):
        src = lax.rem(pairs[0, k], src_tiles)
        tgt = lax.rem(pairs[1, k], tgt_tiles)
        tops = [jnp.full((8, BAND), FLOOR, jnp.float32)] * bands
        sums = [jnp.zeros((8, BAND), jnp.float32)] * bands
        for band in range(bands):
            row_pot = down(rows[src, :, lanes(band)])
            for strip in range(bands):
                score = (row_pot - scaled(held, k, band, strip)).reshape(-1, 8, BAND)
                top = jnp.maximum(tops[strip], jnp.max(score, axis=0))
                sums[strip] = sums[strip] * jnp.exp2(tops[strip] - top) + jnp.sum(jnp.exp2(score - top[None]), axis=0)
                tops[strip] = top
        for strip in range(bands):
            top = jnp.max(tops[strip], axis=0, keepdims=True)
            total = jnp.sum(sums[strip] * jnp.exp2(tops[strip] - top), axis=0, keepdims=True)
            where = (tgt, slice(None), lanes(strip))
            found[where] = log_sum([found[where], top + jnp.log2(total)])
        return carry

    lax.fori_loop(0, count, visit, 0)
    gather(out, found)


def later_rows(edge, src_tiles, tgt_tiles, pairs, counts, held, rows, p0, p1, p2, p3, mass, out, cols, found):
    count = counts[0]
    found[...] = jnp.zeros(found.shape, jnp.float32)
    spread(cols, jnp.log2(stacked(mass)) - log_sum_refs((p0, p1, p2, p3)))
    bands = edge // BAND

    def visit(k, carry):
        src = lax.rem(pairs[0, k], src_tiles)
        tgt = lax.rem(pairs[1, k], tgt_tiles)
        for band in range(bands):
            row_pot = down(rows[src, :, lanes(band)])
            total = 0.0
            for strip in range(bands):
                pot = row_pot + cols[tgt, :, lanes(strip)]
                total = total + jnp.exp2(pot - scaled(held, k, band, strip))
            where = (src, slice(None), lanes(band))
            found[where] = found[where] + across(total)
        return carry

    lax.fori_loop(0, count, visit, 0)
    gather(out, found)


def later_columns(edge, src_tiles, tgt_tiles, pairs, counts, held, rows, cols, p0, p1, p2, p3, mass, out, new_rows, found):
    count = counts[0]
    found[...] = jnp.zeros(found.shape, jnp.float32)
    advance(new_rows, rows, jnp.log2(stacked(mass)) - jnp.log2(p0[...] + p1[...] + p2[...] + p3[...]))
    bands = edge // BAND

    def visit(k, carry):
        src = lax.rem(pairs[0, k], src_tiles)
        tgt = lax.rem(pairs[1, k], tgt_tiles)
        sums = [jnp.zeros((8, BAND), jnp.float32)] * bands
        for band in range(bands):
            row_pot = down(new_rows[src, :, lanes(band)])
            for strip in range(bands):
                pot = row_pot + cols[tgt, :, lanes(strip)]
                sums[strip] = sums[strip] + fold(jnp.exp2(pot - scaled(held, k, band, strip)))
        for strip in range(bands):
            where = (tgt, slice(None), lanes(strip))
            found[where] = found[where] + jnp.sum(sums[strip], axis=0, keepdims=True)
        return carry

    lax.fori_loop(0, count, visit, 0)
    gather(out, found)


def map_tiles(edge, src_tiles, tgt_tiles, core_axis, pairs, counts, held, rows, cols, p0, p1, p2, p3, mass, targets,
              mine, other, new_cols, total):
    count = counts[0]
    total[...] = jnp.zeros(total.shape, jnp.float32)
    advance(new_cols, cols, jnp.log2(stacked(mass)) - jnp.log2(p0[...] + p1[...] + p2[...] + p3[...]))
    bands = edge // BAND
    dim = targets.shape[0]

    def visit(k, carry):
        src = lax.rem(pairs[0, k], src_tiles)
        tgt = lax.rem(pairs[1, k], tgt_tiles)
        points = targets[:, pl.ds(pl.multiple_of(tgt * edge, edge), edge)]
        for pair in range(bands // 2):
            rounded = []
            sums = []
            for band in (2 * pair, 2 * pair + 1):
                row_pot = down(rows[src, :, lanes(band)])
                weights = [
                    jnp.exp2(row_pot + new_cols[tgt, :, lanes(strip)] - scaled(held, k, band, strip))
                    for strip in range(bands)
                ]
                sums.append(across(sum(weights)))
                rounded.append(jnp.concatenate([w.astype(jnp.bfloat16) for w in weights], axis=1))
            both = jnp.concatenate(rounded, axis=0)
            part = lax.dot_general(points, both, (((1,), (1,)), ((), ())), preferred_element_type=jnp.float32)
            where = pl.ds(pl.multiple_of(src * edge + pair * 2 * BAND, 2 * BAND), 2 * BAND)
            total[0:dim, where] = total[0:dim, where] + part
            total[dim:dim + 1, where] = total[dim:dim + 1, where] + jnp.concatenate(sums, axis=1)
        return carry

    lax.fori_loop(0, count, visit, 0)
    share = mine.shape[2]
    core = lax.rem(lax.axis_index(core_axis), 2)
    for z in range(mine.shape[0]):
        own = pl.ds(pl.multiple_of((2 * z + core) * share, BAND), share)
        mine[z] = total[:, own]
        far = pl.ds(pl.multiple_of((2 * z + 1 - core) * share, BAND), share)
        split_mass(other, z, total[0:dim, far], total[dim:dim + 1, far])


def split_mass(ref, z, numer, mass):
    dim = numer.shape[0]
    ref[z, 0:dim] = numer.astype(jnp.bfloat16)
    high = mass.astype(jnp.bfloat16)
    low = (mass - high.astype(jnp.float32)).astype(jnp.bfloat16)
    row = lax.broadcasted_iota(jnp.int32, (8, mass.shape[1]), 0)
    tail = jnp.where(row == 0, high.astype(jnp.float32), jnp.where(row == 1, low.astype(jnp.float32), 0.0))
    ref[z, dim:dim + 8] = tail.astype(jnp.bfloat16)


def join_pair(dim, mine, got, out):
    for z in range(mine.shape[0]):
        arrived = got[z].astype(jnp.float32)
        numer = mine[z, 0:dim] + arrived[0:dim]
        mass = mine[z, dim:dim + 1] + arrived[dim:dim + 1] + arrived[dim + 1:dim + 2]
        split_mass(out, z, numer, mass)


def finish(dim, parts, out):
    total = parts[0].astype(jnp.float32)
    for z in range(1, parts.shape[0]):
        total = total + parts[z].astype(jnp.float32)
    out[...] = total[0:dim] / (total[dim:dim + 1] + total[dim + 1:dim + 2])


def exchange(array, axis, distances):
    size = lax.axis_size(axis)
    return [lax.ppermute(array, axis, [(i, i ^ d) for i in range(size)]) for d in distances]


def quarters(array, axis, combine):
    array = combine([array, *exchange(array, axis, (1, 2, 3))])
    return [array, *exchange(array, axis, (4, 8, 12))]


def local(tile_cost, tile_pairs, tile_counts, src_mass, tgt_mass, targets_t):
    slots, edge = tile_cost.shape[0], tile_cost.shape[1]
    src_tiles = src_mass.shape[0] // edge
    tgt_tiles = tgt_mass.shape[0] // edge
    dim = targets_t.shape[0]
    group = lax.axis_size("tgt")
    src_mass = src_mass.reshape(src_tiles, 1, edge)
    tgt_mass = tgt_mass.reshape(tgt_tiles, 1, edge)
    smem = pl.BlockSpec(memory_space=pltpu.SMEM)
    vmem = pl.BlockSpec(memory_space=pltpu.VMEM)
    hbm = pl.BlockSpec(memory_space=pltpu.HBM)
    by_src = jax.ShapeDtypeStruct((src_tiles, edge), jnp.float32)
    by_tgt = jax.ShapeDtypeStruct((tgt_tiles, edge), jnp.float32)
    src_rows = jax.ShapeDtypeStruct((src_tiles, 1, edge), jnp.float32)
    tgt_rows = jax.ShapeDtypeStruct((tgt_tiles, 1, edge), jnp.float32)
    src_found = [pltpu.VMEM(src_rows.shape, jnp.float32)]
    tgt_found = [pltpu.VMEM(tgt_rows.shape, jnp.float32)]
    index = (tile_pairs.T, tile_counts)
    held_type = pltpu.VMEM(tile_cost.shape, tile_cost.dtype)

    def over_tiles(body, costs, outs, operands, scratch, costs_in=vmem, vmem_mib=10):
        return pl.pallas_call(
            body,
            out_shape=outs,
            in_specs=[smem, smem, costs_in] + [vmem] * len(operands),
            out_specs=jax.tree.map(lambda _: vmem, outs),
            scratch_shapes=scratch,
            compiler_params=pltpu.CompilerParams(vmem_limit_bytes=vmem_mib << 20),
        )(*index, costs, *operands)

    small = pltpu.CompilerParams(vmem_limit_bytes=6 << 20)
    sizes = (edge, src_tiles, tgt_tiles)
    row_part, held = over_tiles(
        functools.partial(first_rows, edge, src_tiles),
        pltpu.with_memory_space_constraint(tile_cost, pltpu.HBM),
        (by_src, held_type),
        (),
        [*src_found, pltpu.SemaphoreType.DMA((slots,))],
        hbm,
    )
    held = pltpu.with_memory_space_constraint(held, pltpu.VMEM)
    row_parts = quarters(row_part, "tgt", log_sum)
    col_part, rows = over_tiles(functools.partial(first_columns, *sizes), held, (by_tgt, src_rows), (*row_parts, src_mass), tgt_found)
    col_parts = quarters(col_part, "src", log_sum)
    row_part, cols = over_tiles(functools.partial(later_rows, *sizes), held, (by_src, tgt_rows), (rows, *col_parts, tgt_mass), src_found)
    row_parts = quarters(row_part, "tgt", sum)
    col_part, rows = over_tiles(
        functools.partial(later_columns, *sizes), held, (by_tgt, src_rows), (rows, cols, *row_parts, src_mass), tgt_found
    )
    col_parts = quarters(col_part, "src", sum)
    share = src_mass.size // group
    half = group // 2
    wire = jax.ShapeDtypeStruct((half, dim + 8, share), jnp.bfloat16)
    mine, other = over_tiles(
        functools.partial(map_tiles, *sizes, "tgt"),
        held,
        (jax.ShapeDtypeStruct((half, dim + 8, share), jnp.float32), wire),
        (rows, cols, *col_parts, tgt_mass, targets_t),
        [*tgt_found, pltpu.VMEM((dim + 8, src_mass.size), jnp.float32)],
        vmem_mib=16,
    )
    (got,) = exchange(other, "tgt", (1,))
    joined = pl.pallas_call(
        functools.partial(join_pair, dim), out_shape=wire, in_specs=[vmem] * 2, out_specs=vmem, compiler_params=small
    )(mine, got)
    parts = lax.all_to_all(
        joined, "tgt", 0, 0, axis_index_groups=[[2 * z + c for z in range(half)] for c in range(2)]
    )
    return pl.pallas_call(
        functools.partial(finish, dim),
        out_shape=jax.ShapeDtypeStruct((dim, share), jnp.float32),
        in_specs=[vmem],
        out_specs=vmem,
        compiler_params=small,
    )(parts)


def solution(mesh):
    return jax.shard_map(
        local,
        mesh=mesh,
        in_specs=(
            P(("src", "tgt"), None, None),
            P(("src", "tgt"), None),
            P(("src", "tgt")),
            P("src"),
            P("tgt"),
            P(None, "tgt"),
        ),
        out_specs=P(None, ("src", "tgt")),
        check_vma=False,
    )
```

```python
import functools
import math

import jax
import jax.numpy as jnp
from jax import lax
from jax.experimental import pallas as pl
from jax.experimental.pallas import tpu as pltpu
from jax.sharding import PartitionSpec as P

ENTROPIC = 0.02
SCALE = math.log2(math.e) / ENTROPIC
FLOOR = -1e30
BAND = 128


def log_sum(parts):
    top = functools.reduce(jnp.maximum, parts)
    total = sum(jnp.exp2(part - top) for part in parts)
    return top + jnp.log2(total)


def lanes(k):
    return slice(k * BAND, (k + 1) * BAND)


def groups(k):
    return slice(k * 8, (k + 1) * 8)


def down(row):
    return jnp.broadcast_to(row, (BAND, BAND)).T


def across(block):
    return jnp.sum(block.T, axis=0, keepdims=True)


def by_eight(block):
    return block.reshape(-1, 8, BAND)


def stacked(ref):
    return jnp.concatenate([ref[k] for k in range(ref.shape[0])], axis=0)


def spread(ref, block):
    for k in range(ref.shape[0]):
        ref[k] = block[k:k + 1]


def gather(ref, rows):
    for k in range(ref.shape[0]):
        ref[k:k + 1] = rows[k]


def first_rows(edge, tiles, pairs_hbm, src_mass_hbm, tgt_mass_hbm, costs,
               out, scores, pairs, counts, src_mass, tgt_mass, held, found, small_sems, sems):
    slots = costs.shape[0]
    moves = ((pairs_hbm, pairs), (src_mass_hbm, src_mass), (tgt_mass_hbm, tgt_mass))
    small = [pltpu.make_async_copy(*move, small_sems.at[k]) for k, move in enumerate(moves)]
    for copy in small[:1]:
        copy.start()
    for k in range(slots):
        pltpu.make_async_copy(costs.at[k], held.at[k], sems.at[k]).start()
    for copy in small[1:]:
        copy.start()
    found[...] = jnp.full(found.shape, FLOOR, jnp.float32)
    bands = edge // BAND
    piece = BAND // 4
    for copy in small[:1]:
        copy.wait()
    count = 1
    for k in range(1, slots):
        differs = jnp.logical_or(pairs[0, k] != pairs[0, 0], pairs[1, k] != pairs[1, 0])
        count = count + differs.astype(jnp.int32)
    counts[0] = count

    def scan(k):
        pltpu.make_async_copy(costs.at[k], held.at[k], sems.at[k]).wait()
        parts = []
        for band in range(bands):
            lows, totals = [], []
            for quarter in range(4):
                rows = pl.ds(band * BAND + quarter * piece, piece)
                blocks = []
                for strip in range(bands):
                    block = held[k, rows, lanes(strip)].astype(jnp.float32) * SCALE
                    scores[k, rows, lanes(strip)] = block
                    blocks.append(block)
                low = functools.reduce(jnp.minimum, blocks)
                totals.append(sum(jnp.exp2(low - block) for block in blocks))
                lows.append(low)
            low = jnp.concatenate(lows, axis=0).T
            least = jnp.min(low, axis=0, keepdims=True)
            total = jnp.sum(jnp.concatenate(totals, axis=0).T * jnp.exp2(least - low), axis=0, keepdims=True)
            parts.append(jnp.where(k < count, jnp.log2(total) - least, FLOOR))
        return parts

    def visit(step, carry):
        pair = (2 * step, 2 * step + 1)
        for k, parts in zip(pair, [scan(k) for k in pair], strict=True):
            for band, part in enumerate(parts):
                where = (lax.rem(pairs[0, k], tiles), slice(None), lanes(band))
                found[where] = log_sum([found[where], part])
        return carry

    steps = lax.div(count + 1, 2)
    lax.fori_loop(0, steps, visit, 0)

    def drain(k, carry):
        pltpu.make_async_copy(costs.at[k], held.at[k], sems.at[k]).wait()
        return carry

    lax.fori_loop(2 * steps, slots, drain, 0)
    for copy in small[1:]:
        copy.wait()
    gather(out, found)


def first_columns(edge, src_tiles, tgt_tiles, pairs, counts, scores, parts, mass, out, plan, tops, rows, found):
    found[...] = jnp.full(found.shape, FLOOR, jnp.float32)
    spread(rows, jnp.log2(stacked(mass)) - log_sum([part[...] for part in parts]))
    bands = edge // BAND
    count = counts[0]

    def scan(k):
        src = lax.rem(pairs[0, k], src_tiles)
        peaks = [[] for _ in range(bands)]
        sums = [[] for _ in range(bands)]
        for band in range(bands):
            row_pot = down(rows[src, :, lanes(band)])
            for strip in range(bands):
                score = by_eight(row_pot - scores[k, lanes(band), lanes(strip)])
                peak = jnp.max(score, axis=0)
                value = jnp.exp2(score - peak[None])
                plan[k, lanes(band), lanes(strip)] = value.reshape(BAND, BAND)
                tops[k, groups(band), lanes(strip)] = peak
                peaks[strip].append(peak)
                sums[strip].append(jnp.sum(value, axis=0))
        results = []
        for strip in range(bands):
            peak = functools.reduce(jnp.maximum, peaks[strip])
            top = jnp.max(peak, axis=0, keepdims=True)
            total = sum(part * jnp.exp2(at - top) for part, at in zip(sums[strip], peaks[strip], strict=True))
            total = jnp.sum(total, axis=0, keepdims=True)
            results.append(jnp.where(k < count, top + jnp.log2(total), FLOOR))
        return results

    def visit(step, carry):
        pair = (2 * step, 2 * step + 1)
        for k, results in zip(pair, [scan(k) for k in pair], strict=True):
            for strip, result in enumerate(results):
                where = (lax.rem(pairs[1, k], tgt_tiles), slice(None), lanes(strip))
                found[where] = log_sum([found[where], result])
        return carry

    lax.fori_loop(0, lax.div(count + 1, 2), visit, 0)
    gather(out, found)


def later_rows(edge, src_tiles, tgt_tiles, pairs, counts, plan, tops, parts, mass, out, scale, cols, found):
    found[...] = jnp.zeros(found.shape, jnp.float32)
    spread(cols, jnp.log2(stacked(mass)) - log_sum([part[...] for part in parts]))
    bands = edge // BAND
    count = counts[0]

    def scan(k):
        tgt = lax.rem(pairs[1, k], tgt_tiles)
        results = []
        for band in range(bands):
            total = 0.0
            for strip in range(bands):
                factor = jnp.exp2(tops[k, groups(band), lanes(strip)] + cols[tgt, :, lanes(strip)])
                factor = jnp.where(k < count, factor, 0.0)
                scale[k, groups(band), lanes(strip)] = factor
                total = total + by_eight(plan[k, lanes(band), lanes(strip)]) * factor[None]
            results.append(across(total.reshape(BAND, BAND)))
        return results

    def visit(step, carry):
        pair = (2 * step, 2 * step + 1)
        for k, results in zip(pair, [scan(k) for k in pair], strict=True):
            for band, result in enumerate(results):
                where = (lax.rem(pairs[0, k], src_tiles), slice(None), lanes(band))
                found[where] = found[where] + result
        return carry

    lax.fori_loop(0, lax.div(count + 1, 2), visit, 0)
    gather(out, found)


def later_columns(edge, src_tiles, tgt_tiles, pairs, counts, plan, scale, parts, mass, out, rows, found):
    found[...] = jnp.zeros(found.shape, jnp.float32)
    spread(rows, stacked(mass) / sum(part[...] for part in parts))
    bands = edge // BAND

    def scan(k):
        src = lax.rem(pairs[0, k], src_tiles)
        sums = [0.0] * bands
        for band in range(bands):
            row_scale = by_eight(down(rows[src, :, lanes(band)]))
            for strip in range(bands):
                part = jnp.sum(by_eight(plan[k, lanes(band), lanes(strip)]) * row_scale, axis=0)
                sums[strip] = sums[strip] + part * scale[k, groups(band), lanes(strip)]
        return [jnp.sum(part, axis=0, keepdims=True) for part in sums]

    def visit(step, carry):
        pair = (2 * step, 2 * step + 1)
        for k, results in zip(pair, [scan(k) for k in pair], strict=True):
            for strip, result in enumerate(results):
                where = (lax.rem(pairs[1, k], tgt_tiles), slice(None), lanes(strip))
                found[where] = found[where] + result
        return carry

    lax.fori_loop(0, lax.div(counts[0] + 1, 2), visit, 0)
    gather(out, found)


def map_tiles(edge, src_tiles, tgt_tiles, pairs, counts, plan, scale, rows, parts, mass, targets, mine, other,
              cols, total, even, odd):
    total[...] = jnp.zeros(total.shape, jnp.float32)
    spread(cols, stacked(mass) / sum(part[...] for part in parts))
    bands = edge // BAND
    dim = targets.shape[0]

    def weigh(k, rounded):
        src = lax.rem(pairs[0, k], src_tiles)
        tgt = lax.rem(pairs[1, k], tgt_tiles)
        for band in range(bands):
            row_scale = by_eight(down(rows[src, :, lanes(band)]))
            mass_sum = 0.0
            for strip in range(bands):
                factor = scale[k, groups(band), lanes(strip)] * cols[tgt, :, lanes(strip)]
                weight = (by_eight(plan[k, lanes(band), lanes(strip)]) * factor[None] * row_scale).reshape(BAND, BAND)
                mass_sum = mass_sum + weight
                rounded[lanes(band), lanes(strip)] = weight.astype(jnp.bfloat16)
            where = pl.ds(pl.multiple_of(src * edge + band * BAND, BAND), BAND)
            total[dim:dim + 1, where] = total[dim:dim + 1, where] + across(mass_sum)

    def apply(k, rounded):
        src = lax.rem(pairs[0, k], src_tiles)
        tgt = lax.rem(pairs[1, k], tgt_tiles)
        points = targets[:, pl.ds(pl.multiple_of(tgt * edge, edge), edge)]
        part = lax.dot_general(points, rounded[...], (((1,), (1,)), ((), ())), preferred_element_type=jnp.float32)
        where = pl.ds(pl.multiple_of(src * edge, edge), edge)
        total[0:dim, where] = total[0:dim, where] + part

    def visit(step, carry):
        weigh(2 * step, even)
        weigh(2 * step + 1, odd)
        apply(2 * step, even)
        apply(2 * step + 1, odd)
        return carry

    lax.fori_loop(0, lax.div(counts[0] + 1, 2), visit, 0)
    share = mine.shape[2]
    core = lax.rem(lax.axis_index("tgt"), 2)
    for z in range(mine.shape[0]):
        own = pl.ds(pl.multiple_of((2 * z + core) * share, BAND), share)
        mine[z] = total[:, own]
        far = pl.ds(pl.multiple_of((2 * z + 1 - core) * share, BAND), share)
        split_mass(other, z, total[0:dim, far], total[dim:dim + 1, far])


def split_mass(ref, z, numer, mass):
    dim = numer.shape[0]
    ref[z, 0:dim] = numer.astype(jnp.bfloat16)
    high = mass.astype(jnp.bfloat16)
    low = (mass - high.astype(jnp.float32)).astype(jnp.bfloat16)
    row = lax.broadcasted_iota(jnp.int32, (8, mass.shape[1]), 0)
    tail = jnp.where(row == 0, high.astype(jnp.float32), jnp.where(row == 1, low.astype(jnp.float32), 0.0))
    ref[z, dim:dim + 8] = tail.astype(jnp.bfloat16)


def join_pair(dim, axis, mine, got, *outs):
    chips = mine.shape[0]
    here = lax.div(lax.axis_index(axis), 2)
    for k, out in enumerate(outs):
        z = lax.rem(here + chips - k, chips)
        arrived = got[z].astype(jnp.float32)
        numer = mine[z, 0:dim] + arrived[0:dim]
        mass = mine[z, dim:dim + 1] + arrived[dim:dim + 1] + arrived[dim + 1:dim + 2]
        split_mass(out, 0, numer, mass)


def finish(dim, *refs):
    *parts, out = refs
    total = sum(part[0].astype(jnp.float32) for part in parts)
    out[...] = total[0:dim] / (total[dim:dim + 1] + total[dim + 1:dim + 2])


def exchange(array, axis, distances):
    size = lax.axis_size(axis)
    return [lax.ppermute(array, axis, [(i, i ^ d) for i in range(size)]) for d in distances]


def ahead(array, axis, chips):
    size = lax.axis_size(axis)
    return lax.ppermute(array, axis, [((i + 2 * chips) % size, i) for i in range(size)])


def over_torus(array, axis, combine):
    array = combine([array, *exchange(array, axis, (1, 2, 3))])
    return [array, *exchange(array, axis, (4, 8, 12))]


def over_ring(array, axis, combine):
    one = combine([array, *exchange(array, axis, (1,))])
    two = combine([one, ahead(one, axis, 1)])
    return [two, ahead(two, axis, 3), ahead(two, axis, -2), ahead(one, axis, 2), ahead(one, axis, -3)]


def local(tile_cost, tile_pairs, tile_counts, src_mass, tgt_mass, targets_t):
    slots, edge = tile_cost.shape[0], tile_cost.shape[1]
    src_tiles = src_mass.shape[0] // edge
    tgt_tiles = tgt_mass.shape[0] // edge
    dim = targets_t.shape[0]
    group = lax.axis_size("tgt")
    src_mass = src_mass.reshape(src_tiles, 1, edge)
    tgt_mass = tgt_mass.reshape(tgt_tiles, 1, edge)
    smem = pl.BlockSpec(memory_space=pltpu.SMEM)
    vmem = pl.BlockSpec(memory_space=pltpu.VMEM)
    hbm = pl.BlockSpec(memory_space=pltpu.HBM)
    by_src = jax.ShapeDtypeStruct((src_tiles, edge), jnp.float32)
    by_tgt = jax.ShapeDtypeStruct((tgt_tiles, edge), jnp.float32)
    src_rows = (src_tiles, 1, edge)
    tgt_rows = (tgt_tiles, 1, edge)
    full = pltpu.VMEM(tile_cost.shape, jnp.float32)
    tall = pltpu.VMEM((slots, edge // BAND * 8, edge), jnp.float32)
    pairs = tile_pairs.T
    sizes = (edge, src_tiles, tgt_tiles)

    def limit(mib):
        return pltpu.CompilerParams(vmem_limit_bytes=mib << 20)

    def over_tiles(body, operands, outs, scratch, mib=6, extra=()):
        return pl.pallas_call(
            functools.partial(body, *sizes),
            out_shape=outs,
            in_specs=[smem, smem, *jax.tree.map(lambda _: vmem, operands)],
            out_specs=jax.tree.map(lambda _: vmem, outs),
            scratch_shapes=[pltpu.VMEM(shape, jnp.float32) for shape in scratch] + list(extra),
            compiler_params=limit(mib),
        )(pairs, counts, *operands)

    small = limit(6)
    inputs = (pairs, src_mass, tgt_mass, tile_cost)
    row_part, scores, pairs, counts, src_mass, tgt_mass = pl.pallas_call(
        functools.partial(first_rows, edge, src_tiles),
        out_shape=(
            by_src,
            full,
            pltpu.SMEM(pairs.shape, jnp.int32),
            pltpu.SMEM(tile_counts.shape, jnp.int32),
            pltpu.VMEM(src_rows, jnp.float32),
            pltpu.VMEM(tgt_rows, jnp.float32),
        ),
        in_specs=[hbm] * 4,
        out_specs=(vmem, vmem, smem, smem, vmem, vmem),
        scratch_shapes=[
            pltpu.VMEM(tile_cost.shape, tile_cost.dtype),
            pltpu.VMEM(src_rows, jnp.float32),
            pltpu.SemaphoreType.DMA((3,)),
            pltpu.SemaphoreType.DMA((slots,)),
        ],
        compiler_params=limit(10),
    )(*[pltpu.with_memory_space_constraint(array, pltpu.HBM) for array in inputs])
    row_parts = over_ring(row_part, "tgt", log_sum)
    col_part, plan, tops = over_tiles(
        first_columns, (scores, row_parts, src_mass), (by_tgt, full, tall), [src_rows, tgt_rows]
    )
    col_parts = over_torus(col_part, "src", log_sum)
    row_part, scale = over_tiles(
        later_rows, (plan, tops, col_parts, tgt_mass), (by_src, tall), [tgt_rows, src_rows]
    )
    row_parts = over_ring(row_part, "tgt", sum)
    col_part, rows = over_tiles(
        later_columns,
        (plan, scale, row_parts, src_mass),
        (by_tgt, jax.ShapeDtypeStruct(src_rows, jnp.float32)),
        [tgt_rows],
    )
    col_parts = over_torus(col_part, "src", sum)
    share = src_mass.size // group
    half = group // 2
    wire = jax.ShapeDtypeStruct((half, dim + 8, share), jnp.bfloat16)
    mine, other = over_tiles(
        map_tiles,
        (plan, scale, rows, col_parts, tgt_mass, targets_t),
        (jax.ShapeDtypeStruct((half, dim + 8, share), jnp.float32), wire),
        [tgt_rows, (dim + 8, src_mass.size)],
        16,
        [pltpu.VMEM((edge, edge), jnp.bfloat16)] * 2,
    )
    (got,) = exchange(other, "tgt", (1,))
    block = jax.ShapeDtypeStruct((1, *wire.shape[1:]), wire.dtype)
    joined = pl.pallas_call(
        functools.partial(join_pair, dim, "tgt"),
        out_shape=[block] * half,
        in_specs=[vmem] * 2,
        out_specs=[vmem] * half,
        compiler_params=small,
    )(mine, got)
    order = sorted(range(1, half), key=lambda k: -min(k, half - k))
    parts = [joined[0], *[ahead(joined[k], "tgt", k) for k in order]]
    return pl.pallas_call(
        functools.partial(finish, dim),
        out_shape=jax.ShapeDtypeStruct((dim, share), jnp.float32),
        in_specs=[vmem] * half,
        out_specs=vmem,
        compiler_params=small,
    )(*parts)


def solution(mesh):
    return jax.shard_map(
        local,
        mesh=mesh,
        in_specs=(
            P(("src", "tgt"), None, None),
            P(("src", "tgt"), None),
            P(("src", "tgt")),
            P("src"),
            P("tgt"),
            P(None, "tgt"),
        ),
        out_specs=P(None, ("src", "tgt")),
        check_vma=False,
    )
```

```python
import functools
import math

import jax
import jax.numpy as jnp
from jax import lax
from jax.experimental import pallas as pl
from jax.experimental.pallas import tpu as pltpu
from jax.sharding import PartitionSpec as P

ENTROPIC = 0.02
SCALE = math.log2(math.e) / ENTROPIC
FLOOR = -1e30
BAND = 128


def log_sum(parts):
    top = functools.reduce(jnp.maximum, parts)
    total = sum(jnp.exp2(part - top) for part in parts)
    return top + jnp.log2(total)


def lanes(k):
    return slice(k * BAND, (k + 1) * BAND)


def groups(k):
    return slice(k * 8, (k + 1) * 8)


def down(row):
    return jnp.broadcast_to(row, (BAND, BAND)).T


def across(block):
    return jnp.sum(block.T, axis=0, keepdims=True)


def by_eight(block):
    return block.reshape(-1, 8, BAND)


def stacked(ref):
    return jnp.concatenate([ref[k] for k in range(ref.shape[0])], axis=0)


def spread(ref, block):
    for k in range(ref.shape[0]):
        ref[k] = block[k:k + 1]


def gather(ref, rows):
    for k in range(ref.shape[0]):
        ref[k:k + 1] = rows[k]


def first_rows(edge, tiles, pairs_hbm, src_mass_hbm, tgt_mass_hbm, costs,
               out, scores, pairs, counts, src_mass, tgt_mass, held, found, small_sems, sems):
    slots = costs.shape[0]
    moves = ((pairs_hbm, pairs), (src_mass_hbm, src_mass), (tgt_mass_hbm, tgt_mass))
    small = [pltpu.make_async_copy(*move, small_sems.at[k]) for k, move in enumerate(moves)]
    for copy in small[:1]:
        copy.start()
    for k in range(slots):
        pltpu.make_async_copy(costs.at[k], held.at[k], sems.at[k]).start()
    for copy in small[1:]:
        copy.start()
    found[...] = jnp.full(found.shape, FLOOR, jnp.float32)
    bands = edge // BAND
    piece = BAND // 4
    for copy in small[:1]:
        copy.wait()
    count = 1
    for k in range(1, slots):
        differs = jnp.logical_or(pairs[0, k] != pairs[0, 0], pairs[1, k] != pairs[1, 0])
        count = count + differs.astype(jnp.int32)
    counts[0] = count

    def scan(k):
        pltpu.make_async_copy(costs.at[k], held.at[k], sems.at[k]).wait()
        parts = []
        for band in range(bands):
            lows, totals = [], []
            for quarter in range(4):
                rows = pl.ds(band * BAND + quarter * piece, piece)
                blocks = []
                for strip in range(bands):
                    block = held[k, rows, lanes(strip)].astype(jnp.float32) * SCALE
                    scores[k, rows, lanes(strip)] = block
                    blocks.append(block)
                low = functools.reduce(jnp.minimum, blocks)
                totals.append(sum(jnp.exp2(low - block) for block in blocks))
                lows.append(low)
            low = jnp.concatenate(lows, axis=0).T
            least = jnp.min(low, axis=0, keepdims=True)
            total = jnp.sum(jnp.concatenate(totals, axis=0).T * jnp.exp2(least - low), axis=0, keepdims=True)
            parts.append(jnp.where(k < count, jnp.log2(total) - least, FLOOR))
        return parts

    def visit(step, carry):
        pair = (2 * step, 2 * step + 1)
        for k, parts in zip(pair, [scan(k) for k in pair], strict=True):
            for band, part in enumerate(parts):
                where = (lax.rem(pairs[0, k], tiles), slice(None), lanes(band))
                found[where] = log_sum([found[where], part])
        return carry

    steps = lax.div(count + 1, 2)
    lax.fori_loop(0, steps, visit, 0)

    def drain(k, carry):
        pltpu.make_async_copy(costs.at[k], held.at[k], sems.at[k]).wait()
        return carry

    lax.fori_loop(2 * steps, slots, drain, 0)
    for copy in small[1:]:
        copy.wait()
    gather(out, found)


def first_columns(edge, src_tiles, tgt_tiles, pairs, counts, scores, parts, mass, out, plan, tops, rows, found):
    found[...] = jnp.full(found.shape, FLOOR, jnp.float32)
    spread(rows, jnp.log2(stacked(mass)) - log_sum([part[...] for part in parts]))
    bands = edge // BAND
    count = counts[0]

    def scan(k):
        src = lax.rem(pairs[0, k], src_tiles)
        peaks = [[] for _ in range(bands)]
        sums = [[] for _ in range(bands)]
        for band in range(bands):
            row_pot = down(rows[src, :, lanes(band)])
            for strip in range(bands):
                score = by_eight(row_pot - scores[k, lanes(band), lanes(strip)])
                peak = jnp.max(score, axis=0)
                value = jnp.exp2(score - peak[None])
                plan[k, lanes(band), lanes(strip)] = value.reshape(BAND, BAND)
                tops[k, groups(band), lanes(strip)] = peak
                peaks[strip].append(peak)
                sums[strip].append(jnp.sum(value, axis=0))
        results = []
        for strip in range(bands):
            peak = functools.reduce(jnp.maximum, peaks[strip])
            top = jnp.max(peak, axis=0, keepdims=True)
            total = sum(part * jnp.exp2(at - top) for part, at in zip(sums[strip], peaks[strip], strict=True))
            total = jnp.sum(total, axis=0, keepdims=True)
            results.append(jnp.where(k < count, top + jnp.log2(total), FLOOR))
        return results

    def visit(step, carry):
        pair = (2 * step, 2 * step + 1)
        for k, results in zip(pair, [scan(k) for k in pair], strict=True):
            for strip, result in enumerate(results):
                where = (lax.rem(pairs[1, k], tgt_tiles), slice(None), lanes(strip))
                found[where] = log_sum([found[where], result])
        return carry

    lax.fori_loop(0, lax.div(count + 1, 2), visit, 0)
    gather(out, found)


def later_rows(edge, src_tiles, tgt_tiles, pairs, counts, plan, tops, parts, mass, out, scale, cols, found):
    found[...] = jnp.zeros(found.shape, jnp.float32)
    spread(cols, jnp.log2(stacked(mass)) - log_sum([part[...] for part in parts]))
    bands = edge // BAND
    count = counts[0]

    def scan(k):
        tgt = lax.rem(pairs[1, k], tgt_tiles)
        results = []
        for band in range(bands):
            total = 0.0
            for strip in range(bands):
                factor = jnp.exp2(tops[k, groups(band), lanes(strip)] + cols[tgt, :, lanes(strip)])
                factor = jnp.where(k < count, factor, 0.0)
                scale[k, groups(band), lanes(strip)] = factor
                total = total + by_eight(plan[k, lanes(band), lanes(strip)]) * factor[None]
            results.append(across(total.reshape(BAND, BAND)))
        return results

    def visit(step, carry):
        pair = (2 * step, 2 * step + 1)
        for k, results in zip(pair, [scan(k) for k in pair], strict=True):
            for band, result in enumerate(results):
                where = (lax.rem(pairs[0, k], src_tiles), slice(None), lanes(band))
                found[where] = found[where] + result
        return carry

    lax.fori_loop(0, lax.div(count + 1, 2), visit, 0)
    gather(out, found)


def later_columns(edge, src_tiles, tgt_tiles, pairs, counts, plan, scale, parts, mass, out, rows, found):
    found[...] = jnp.zeros(found.shape, jnp.float32)
    spread(rows, stacked(mass) / sum(part[...] for part in parts))
    bands = edge // BAND

    def scan(k):
        src = lax.rem(pairs[0, k], src_tiles)
        sums = [0.0] * bands
        for band in range(bands):
            row_scale = by_eight(down(rows[src, :, lanes(band)]))
            for strip in range(bands):
                part = jnp.sum(by_eight(plan[k, lanes(band), lanes(strip)]) * row_scale, axis=0)
                sums[strip] = sums[strip] + part * scale[k, groups(band), lanes(strip)]
        return [jnp.sum(part, axis=0, keepdims=True) for part in sums]

    def visit(step, carry):
        pair = (2 * step, 2 * step + 1)
        for k, results in zip(pair, [scan(k) for k in pair], strict=True):
            for strip, result in enumerate(results):
                where = (lax.rem(pairs[1, k], tgt_tiles), slice(None), lanes(strip))
                found[where] = found[where] + result
        return carry

    lax.fori_loop(0, lax.div(counts[0] + 1, 2), visit, 0)
    gather(out, found)


def map_tiles(edge, src_tiles, tgt_tiles, pairs, counts, plan, scale, rows, parts, mass, targets, mine, other,
              cols, total, found, even, odd):
    total[...] = jnp.zeros(total.shape, jnp.float32)
    found[...] = jnp.zeros(found.shape, jnp.float32)
    spread(cols, stacked(mass) / sum(part[...] for part in parts))
    bands = edge // BAND
    dim = targets.shape[0]

    def weigh(k, rounded):
        src = lax.rem(pairs[0, k], src_tiles)
        tgt = lax.rem(pairs[1, k], tgt_tiles)
        for band in range(bands):
            row_scale = by_eight(down(rows[src, :, lanes(band)]))
            mass_sum = 0.0
            for strip in range(bands):
                factor = scale[k, groups(band), lanes(strip)] * cols[tgt, :, lanes(strip)]
                weight = (by_eight(plan[k, lanes(band), lanes(strip)]) * factor[None] * row_scale).reshape(BAND, BAND)
                mass_sum = mass_sum + weight
                rounded[lanes(band), lanes(strip)] = weight.astype(jnp.bfloat16)
            where = (src, slice(None), lanes(band))
            found[where] = found[where] + across(mass_sum)

    def apply(k, rounded):
        src = lax.rem(pairs[0, k], src_tiles)
        tgt = lax.rem(pairs[1, k], tgt_tiles)
        points = targets[:, pl.ds(pl.multiple_of(tgt * edge, edge), edge)]
        part = lax.dot_general(points, rounded[...], (((1,), (1,)), ((), ())), preferred_element_type=jnp.float32)
        where = pl.ds(pl.multiple_of(src * edge, edge), edge)
        total[:, where] = total[:, where] + part

    def visit(step, carry):
        weigh(2 * step, even)
        weigh(2 * step + 1, odd)
        apply(2 * step, even)
        apply(2 * step + 1, odd)
        return carry

    lax.fori_loop(0, lax.div(counts[0] + 1, 2), visit, 0)
    mass_row = jnp.concatenate([found[k] for k in range(src_tiles)], axis=1)
    share = mine.shape[2]
    core = lax.rem(lax.axis_index("tgt"), 2)
    for z in range(mine.shape[0]):
        near, far = (2 * z + core) * share, (2 * z + 1 - core) * share
        halves = [mass_row[:, (2 * z + k) * share:(2 * z + k + 1) * share] for k in range(2)]
        mine[z, 0:dim] = total[:, pl.ds(pl.multiple_of(near, BAND), share)]
        mine[z, dim:dim + 1] = jnp.where(core == 0, halves[0], halves[1])
        split_mass(other, z, total[:, pl.ds(pl.multiple_of(far, BAND), share)], jnp.where(core == 0, halves[1], halves[0]))


def split_mass(ref, z, numer, mass):
    dim = numer.shape[0]
    ref[z, 0:dim] = numer.astype(jnp.bfloat16)
    high = mass.astype(jnp.bfloat16)
    low = (mass - high.astype(jnp.float32)).astype(jnp.bfloat16)
    row = lax.broadcasted_iota(jnp.int32, (8, mass.shape[1]), 0)
    tail = jnp.where(row == 0, high.astype(jnp.float32), jnp.where(row == 1, low.astype(jnp.float32), 0.0))
    ref[z, dim:dim + 8] = tail.astype(jnp.bfloat16)


def join_pair(dim, axis, mine, got, *outs):
    chips = mine.shape[0]
    here = lax.div(lax.axis_index(axis), 2)
    for k, out in enumerate(outs):
        z = lax.rem(here + chips - k, chips)
        arrived = got[z].astype(jnp.float32)
        numer = mine[z, 0:dim] + arrived[0:dim]
        mass = mine[z, dim:dim + 1] + arrived[dim:dim + 1] + arrived[dim + 1:dim + 2]
        split_mass(out, 0, numer, mass)


def finish(dim, *refs):
    *parts, out = refs
    total = sum(part[0].astype(jnp.float32) for part in parts)
    out[...] = total[0:dim] / (total[dim:dim + 1] + total[dim + 1:dim + 2])


def exchange(array, axis, distances):
    size = lax.axis_size(axis)
    return [lax.ppermute(array, axis, [(i, i ^ d) for i in range(size)]) for d in distances]


def ahead(array, axis, chips):
    size = lax.axis_size(axis)
    return lax.ppermute(array, axis, [((i + 2 * chips) % size, i) for i in range(size)])


def over_torus(array, axis, combine):
    array = combine([array, *exchange(array, axis, (1, 2, 3))])
    return [array, *exchange(array, axis, (4, 8, 12))]


def local(tile_cost, tile_pairs, tile_counts, src_mass, tgt_mass, targets_t):
    slots, edge = tile_cost.shape[0], tile_cost.shape[1]
    src_tiles = src_mass.shape[0] // edge
    tgt_tiles = tgt_mass.shape[0] // edge
    dim = targets_t.shape[0]
    group = lax.axis_size("tgt")
    src_mass = src_mass.reshape(src_tiles, 1, edge)
    tgt_mass = tgt_mass.reshape(tgt_tiles, 1, edge)
    smem = pl.BlockSpec(memory_space=pltpu.SMEM)
    vmem = pl.BlockSpec(memory_space=pltpu.VMEM)
    hbm = pl.BlockSpec(memory_space=pltpu.HBM)
    by_src = jax.ShapeDtypeStruct((src_tiles, edge), jnp.float32)
    by_tgt = jax.ShapeDtypeStruct((tgt_tiles, edge), jnp.float32)
    src_rows = (src_tiles, 1, edge)
    tgt_rows = (tgt_tiles, 1, edge)
    full = pltpu.VMEM(tile_cost.shape, jnp.float32)
    tall = pltpu.VMEM((slots, edge // BAND * 8, edge), jnp.float32)
    pairs = tile_pairs.T
    sizes = (edge, src_tiles, tgt_tiles)

    def limit(mib):
        return pltpu.CompilerParams(vmem_limit_bytes=mib << 20)

    def over_tiles(body, operands, outs, scratch, mib=6, extra=()):
        return pl.pallas_call(
            functools.partial(body, *sizes),
            out_shape=outs,
            in_specs=[smem, smem, *jax.tree.map(lambda _: vmem, operands)],
            out_specs=jax.tree.map(lambda _: vmem, outs),
            scratch_shapes=[pltpu.VMEM(shape, jnp.float32) for shape in scratch] + list(extra),
            compiler_params=limit(mib),
        )(pairs, counts, *operands)

    small = limit(6)
    inputs = (pairs, src_mass, tgt_mass, tile_cost)
    row_part, scores, pairs, counts, src_mass, tgt_mass = pl.pallas_call(
        functools.partial(first_rows, edge, src_tiles),
        out_shape=(
            by_src,
            full,
            pltpu.SMEM(pairs.shape, jnp.int32),
            pltpu.SMEM(tile_counts.shape, jnp.int32),
            pltpu.VMEM(src_rows, jnp.float32),
            pltpu.VMEM(tgt_rows, jnp.float32),
        ),
        in_specs=[hbm] * 4,
        out_specs=(vmem, vmem, smem, smem, vmem, vmem),
        scratch_shapes=[
            pltpu.VMEM(tile_cost.shape, tile_cost.dtype),
            pltpu.VMEM(src_rows, jnp.float32),
            pltpu.SemaphoreType.DMA((3,)),
            pltpu.SemaphoreType.DMA((slots,)),
        ],
        compiler_params=limit(10),
    )(*[pltpu.with_memory_space_constraint(array, pltpu.HBM) for array in inputs])
    row_parts = over_torus(row_part, "tgt", log_sum)
    col_part, plan, tops = over_tiles(
        first_columns, (scores, row_parts, src_mass), (by_tgt, full, tall), [src_rows, tgt_rows]
    )
    col_parts = over_torus(col_part, "src", log_sum)
    row_part, scale = over_tiles(
        later_rows, (plan, tops, col_parts, tgt_mass), (by_src, tall), [tgt_rows, src_rows]
    )
    row_parts = over_torus(row_part, "tgt", sum)
    col_part, rows = over_tiles(
        later_columns,
        (plan, scale, row_parts, src_mass),
        (by_tgt, jax.ShapeDtypeStruct(src_rows, jnp.float32)),
        [tgt_rows],
    )
    col_parts = over_torus(col_part, "src", sum)
    share = src_mass.size // group
    half = group // 2
    wire = jax.ShapeDtypeStruct((half, dim + 8, share), jnp.bfloat16)
    mine, other = over_tiles(
        map_tiles,
        (plan, scale, rows, col_parts, tgt_mass, targets_t),
        (jax.ShapeDtypeStruct((half, dim + 8, share), jnp.float32), wire),
        [tgt_rows, (dim, src_mass.size), src_rows],
        16,
        [pltpu.VMEM((edge, edge), jnp.bfloat16)] * 2,
    )
    (got,) = exchange(other, "tgt", (1,))
    block = jax.ShapeDtypeStruct((1, *wire.shape[1:]), wire.dtype)
    joined = pl.pallas_call(
        functools.partial(join_pair, dim, "tgt"),
        out_shape=[block] * half,
        in_specs=[vmem] * 2,
        out_specs=[vmem] * half,
        compiler_params=small,
    )(mine, got)
    order = sorted(range(1, half), key=lambda k: -min(k, half - k))
    parts = [joined[0], *[ahead(joined[k], "tgt", k) for k in order]]
    return pl.pallas_call(
        functools.partial(finish, dim),
        out_shape=jax.ShapeDtypeStruct((dim, share), jnp.float32),
        in_specs=[vmem] * half,
        out_specs=vmem,
        compiler_params=small,
    )(*parts)


def solution(mesh):
    return jax.shard_map(
        local,
        mesh=mesh,
        in_specs=(
            P(("src", "tgt"), None, None),
            P(("src", "tgt"), None),
            P(("src", "tgt")),
            P("src"),
            P("tgt"),
            P(None, "tgt"),
        ),
        out_specs=P(None, ("src", "tgt")),
        check_vma=False,
    )
```

```python
import functools
import math

import jax
import jax.numpy as jnp
from jax import lax
from jax.experimental import pallas as pl
from jax.experimental.pallas import tpu as pltpu
from jax.sharding import PartitionSpec as P

ENTROPIC = 0.02
SCALE = math.log2(math.e) / ENTROPIC
FLOOR = -1e30
BAND = 128


def log_sum(parts):
    top = functools.reduce(jnp.maximum, parts)
    total = sum(jnp.exp2(part - top) for part in parts)
    return top + jnp.log2(total)


def lanes(k):
    return slice(k * BAND, (k + 1) * BAND)


def groups(k):
    return slice(k * 8, (k + 1) * 8)


def down(row):
    return jnp.broadcast_to(row, (BAND, BAND)).T


def across(block):
    return jnp.sum(block.T, axis=0, keepdims=True)


def by_eight(block):
    return block.reshape(-1, 8, BAND)


def stacked(ref):
    return jnp.concatenate([ref[k] for k in range(ref.shape[0])], axis=0)


def spread(ref, block):
    for k in range(ref.shape[0]):
        ref[k] = block[k:k + 1]


def gather(ref, rows):
    for k in range(ref.shape[0]):
        ref[k:k + 1] = rows[k]


def first_rows(edge, tiles, pairs_hbm, src_mass_hbm, tgt_mass_hbm, costs,
               out, scores, pairs, counts, src_mass, tgt_mass, held, found, small_sems, sems):
    slots = costs.shape[0]
    moves = ((pairs_hbm, pairs), (src_mass_hbm, src_mass), (tgt_mass_hbm, tgt_mass))
    small = [pltpu.make_async_copy(*move, small_sems.at[k]) for k, move in enumerate(moves)]
    for copy in small[:1]:
        copy.start()
    for k in range(slots):
        pltpu.make_async_copy(costs.at[k], held.at[k], sems.at[k]).start()
    for copy in small[1:]:
        copy.start()
    found[...] = jnp.full(found.shape, FLOOR, jnp.float32)
    bands = edge // BAND
    piece = BAND // 4
    for copy in small[:1]:
        copy.wait()
    count = 1
    for k in range(1, slots):
        differs = jnp.logical_or(pairs[0, k] != pairs[0, 0], pairs[1, k] != pairs[1, 0])
        count = count + differs.astype(jnp.int32)
    counts[0] = count

    def scan(k):
        pltpu.make_async_copy(costs.at[k], held.at[k], sems.at[k]).wait()
        parts = []
        for band in range(bands):
            lows, totals = [], []
            for quarter in range(4):
                rows = pl.ds(band * BAND + quarter * piece, piece)
                blocks = []
                for strip in range(bands):
                    block = held[k, rows, lanes(strip)].astype(jnp.float32) * SCALE
                    scores[k, rows, lanes(strip)] = block
                    blocks.append(block)
                low = functools.reduce(jnp.minimum, blocks)
                totals.append(sum(jnp.exp2(low - block) for block in blocks))
                lows.append(low)
            low = jnp.concatenate(lows, axis=0).T
            least = jnp.min(low, axis=0, keepdims=True)
            total = jnp.sum(jnp.concatenate(totals, axis=0).T * jnp.exp2(least - low), axis=0, keepdims=True)
            parts.append(jnp.where(k < count, jnp.log2(total) - least, FLOOR))
        return parts

    def visit(step, carry):
        pair = (2 * step, 2 * step + 1)
        for k, parts in zip(pair, [scan(k) for k in pair], strict=True):
            for band, part in enumerate(parts):
                where = (lax.rem(pairs[0, k], tiles), slice(None), lanes(band))
                found[where] = log_sum([found[where], part])
        return carry

    steps = lax.div(count + 1, 2)
    lax.fori_loop(0, steps, visit, 0)

    def drain(k, carry):
        pltpu.make_async_copy(costs.at[k], held.at[k], sems.at[k]).wait()
        return carry

    lax.fori_loop(2 * steps, slots, drain, 0)
    for copy in small[1:]:
        copy.wait()
    gather(out, found)


def first_columns(edge, src_tiles, tgt_tiles, pairs, counts, scores, parts, mass, out, plan, tops, rows, found):
    found[...] = jnp.full(found.shape, FLOOR, jnp.float32)
    spread(rows, jnp.log2(stacked(mass)) - log_sum([part[...] for part in parts]))
    bands = edge // BAND
    count = counts[0]

    def scan(k):
        src = lax.rem(pairs[0, k], src_tiles)
        peaks = [[] for _ in range(bands)]
        sums = [[] for _ in range(bands)]
        for band in range(bands):
            row_pot = down(rows[src, :, lanes(band)])
            for strip in range(bands):
                score = by_eight(row_pot - scores[k, lanes(band), lanes(strip)])
                peak = jnp.max(score, axis=0)
                value = jnp.exp2(score - peak[None])
                plan[k, lanes(band), lanes(strip)] = value.reshape(BAND, BAND)
                tops[k, groups(band), lanes(strip)] = peak
                peaks[strip].append(peak)
                sums[strip].append(jnp.sum(value, axis=0))
        results = []
        for strip in range(bands):
            peak = functools.reduce(jnp.maximum, peaks[strip])
            top = jnp.max(peak, axis=0, keepdims=True)
            total = sum(part * jnp.exp2(at - top) for part, at in zip(sums[strip], peaks[strip], strict=True))
            total = jnp.sum(total, axis=0, keepdims=True)
            results.append(jnp.where(k < count, top + jnp.log2(total), FLOOR))
        return results

    def visit(step, carry):
        pair = (2 * step, 2 * step + 1)
        for k, results in zip(pair, [scan(k) for k in pair], strict=True):
            for strip, result in enumerate(results):
                where = (lax.rem(pairs[1, k], tgt_tiles), slice(None), lanes(strip))
                found[where] = log_sum([found[where], result])
        return carry

    lax.fori_loop(0, lax.div(count + 1, 2), visit, 0)
    gather(out, found)


def later_rows(edge, src_tiles, tgt_tiles, pairs, counts, plan, tops, parts, mass, out, scale, cols, found):
    found[...] = jnp.zeros(found.shape, jnp.float32)
    spread(cols, jnp.log2(stacked(mass)) - log_sum([part[...] for part in parts]))
    bands = edge // BAND
    count = counts[0]

    def scan(k):
        tgt = lax.rem(pairs[1, k], tgt_tiles)
        results = []
        for band in range(bands):
            total = 0.0
            for strip in range(bands):
                factor = jnp.exp2(tops[k, groups(band), lanes(strip)] + cols[tgt, :, lanes(strip)])
                factor = jnp.where(k < count, factor, 0.0)
                scale[k, groups(band), lanes(strip)] = factor
                total = total + by_eight(plan[k, lanes(band), lanes(strip)]) * factor[None]
            results.append(across(total.reshape(BAND, BAND)))
        return results

    def visit(step, carry):
        pair = (2 * step, 2 * step + 1)
        for k, results in zip(pair, [scan(k) for k in pair], strict=True):
            for band, result in enumerate(results):
                where = (lax.rem(pairs[0, k], src_tiles), slice(None), lanes(band))
                found[where] = found[where] + result
        return carry

    lax.fori_loop(0, lax.div(count + 1, 2), visit, 0)
    gather(out, found)


def later_columns(edge, src_tiles, tgt_tiles, pairs, counts, plan, scale, parts, mass, out, rows, found):
    found[...] = jnp.zeros(found.shape, jnp.float32)
    spread(rows, stacked(mass) / sum(part[...] for part in parts))
    bands = edge // BAND

    def scan(k):
        src = lax.rem(pairs[0, k], src_tiles)
        sums = [0.0] * bands
        for band in range(bands):
            row_scale = by_eight(down(rows[src, :, lanes(band)]))
            for strip in range(bands):
                part = jnp.sum(by_eight(plan[k, lanes(band), lanes(strip)]) * row_scale, axis=0)
                sums[strip] = sums[strip] + part * scale[k, groups(band), lanes(strip)]
        return [jnp.sum(part, axis=0, keepdims=True) for part in sums]

    def visit(step, carry):
        pair = (2 * step, 2 * step + 1)
        for k, results in zip(pair, [scan(k) for k in pair], strict=True):
            for strip, result in enumerate(results):
                where = (lax.rem(pairs[1, k], tgt_tiles), slice(None), lanes(strip))
                found[where] = found[where] + result
        return carry

    lax.fori_loop(0, lax.div(counts[0] + 1, 2), visit, 0)
    gather(out, found)


def map_tiles(edge, src_tiles, tgt_tiles, pairs, counts, plan, scale, rows, parts, mass, targets, mine, other,
              cols, total, found, even, odd):
    total[...] = jnp.zeros(total.shape, jnp.float32)
    found[...] = jnp.zeros(found.shape, jnp.float32)
    spread(cols, stacked(mass) / sum(part[...] for part in parts))
    bands = edge // BAND
    dim = targets.shape[0]

    def weigh(k, rounded):
        src = lax.rem(pairs[0, k], src_tiles)
        tgt = lax.rem(pairs[1, k], tgt_tiles)
        for band in range(bands):
            row_scale = by_eight(down(rows[src, :, lanes(band)]))
            mass_sum = 0.0
            for strip in range(bands):
                factor = scale[k, groups(band), lanes(strip)] * cols[tgt, :, lanes(strip)]
                weight = (by_eight(plan[k, lanes(band), lanes(strip)]) * factor[None] * row_scale).reshape(BAND, BAND)
                mass_sum = mass_sum + weight
                rounded[lanes(band), lanes(strip)] = weight.astype(jnp.bfloat16)
            where = (src, slice(None), lanes(band))
            found[where] = found[where] + across(mass_sum)

    def apply(k, rounded):
        src = lax.rem(pairs[0, k], src_tiles)
        tgt = lax.rem(pairs[1, k], tgt_tiles)
        points = targets[:, pl.ds(pl.multiple_of(tgt * edge, edge), edge)]
        part = lax.dot_general(points, rounded[...], (((1,), (1,)), ((), ())), preferred_element_type=jnp.float32)
        where = pl.ds(pl.multiple_of(src * edge, edge), edge)
        total[:, where] = total[:, where] + part

    def visit(step, carry):
        weigh(2 * step, even)
        weigh(2 * step + 1, odd)
        apply(2 * step, even)
        apply(2 * step + 1, odd)
        return carry

    lax.fori_loop(0, lax.div(counts[0] + 1, 2), visit, 0)
    mass_row = jnp.concatenate([found[k] for k in range(src_tiles)], axis=1)
    share = mine.shape[2]
    core = lax.rem(lax.axis_index("tgt"), 2)
    for z in range(mine.shape[0]):
        near, far = (2 * z + core) * share, (2 * z + 1 - core) * share
        halves = [mass_row[:, (2 * z + k) * share:(2 * z + k + 1) * share] for k in range(2)]
        mine[z, 0:dim] = total[:, pl.ds(pl.multiple_of(near, BAND), share)]
        mine[z, dim:dim + 1] = jnp.where(core == 0, halves[0], halves[1])
        split_mass(other, z, total[:, pl.ds(pl.multiple_of(far, BAND), share)], jnp.where(core == 0, halves[1], halves[0]))


def split_mass(ref, z, numer, mass):
    dim = numer.shape[0]
    ref[z, 0:dim] = numer.astype(jnp.bfloat16)
    high = mass.astype(jnp.bfloat16)
    low = (mass - high.astype(jnp.float32)).astype(jnp.bfloat16)
    row = lax.broadcasted_iota(jnp.int32, (8, mass.shape[1]), 0)
    tail = jnp.where(row == 0, high.astype(jnp.float32), jnp.where(row == 1, low.astype(jnp.float32), 0.0))
    ref[z, dim:dim + 8] = tail.astype(jnp.bfloat16)


def join_pair(dim, axis, mine, got, *outs):
    chips = mine.shape[0]
    here = lax.div(lax.axis_index(axis), 2)
    for k, out in enumerate(outs):
        z = lax.rem(here + chips - k, chips)
        arrived = got[z].astype(jnp.float32)
        numer = mine[z, 0:dim] + arrived[0:dim]
        mass = mine[z, dim:dim + 1] + arrived[dim:dim + 1] + arrived[dim + 1:dim + 2]
        split_mass(out, 0, numer, mass)


def finish(dim, *refs):
    *parts, out = refs
    total = sum(part[0].astype(jnp.float32) for part in parts)
    out[...] = total[0:dim] / (total[dim:dim + 1] + total[dim + 1:dim + 2])


def exchange(array, axis, distances):
    size = lax.axis_size(axis)
    return [lax.ppermute(array, axis, [(i, i ^ d) for i in range(size)]) for d in distances]


def ahead(array, axis, chips):
    size = lax.axis_size(axis)
    return lax.ppermute(array, axis, [((i + 2 * chips) % size, i) for i in range(size)])


def over_torus(array, axis, combine):
    array = combine([array, *exchange(array, axis, (1, 2, 3))])
    return [array, *exchange(array, axis, (4, 12, 8))]


def local(tile_cost, tile_pairs, tile_counts, src_mass, tgt_mass, targets_t):
    slots, edge = tile_cost.shape[0], tile_cost.shape[1]
    src_tiles = src_mass.shape[0] // edge
    tgt_tiles = tgt_mass.shape[0] // edge
    dim = targets_t.shape[0]
    group = lax.axis_size("tgt")
    src_mass = src_mass.reshape(src_tiles, 1, edge)
    tgt_mass = tgt_mass.reshape(tgt_tiles, 1, edge)
    smem = pl.BlockSpec(memory_space=pltpu.SMEM)
    vmem = pl.BlockSpec(memory_space=pltpu.VMEM)
    hbm = pl.BlockSpec(memory_space=pltpu.HBM)
    by_src = jax.ShapeDtypeStruct((src_tiles, edge), jnp.float32)
    by_tgt = jax.ShapeDtypeStruct((tgt_tiles, edge), jnp.float32)
    src_rows = (src_tiles, 1, edge)
    tgt_rows = (tgt_tiles, 1, edge)
    full = pltpu.VMEM(tile_cost.shape, jnp.float32)
    tall = pltpu.VMEM((slots, edge // BAND * 8, edge), jnp.float32)
    pairs = tile_pairs.T
    sizes = (edge, src_tiles, tgt_tiles)

    def limit(mib):
        return pltpu.CompilerParams(vmem_limit_bytes=mib << 20)

    def over_tiles(body, operands, outs, scratch, mib=6, extra=()):
        return pl.pallas_call(
            functools.partial(body, *sizes),
            out_shape=outs,
            in_specs=[smem, smem, *jax.tree.map(lambda _: vmem, operands)],
            out_specs=jax.tree.map(lambda _: vmem, outs),
            scratch_shapes=[pltpu.VMEM(shape, jnp.float32) for shape in scratch] + list(extra),
            compiler_params=limit(mib),
        )(pairs, counts, *operands)

    small = limit(6)
    inputs = (pairs, src_mass, tgt_mass, tile_cost)
    row_part, scores, pairs, counts, src_mass, tgt_mass = pl.pallas_call(
        functools.partial(first_rows, edge, src_tiles),
        out_shape=(
            by_src,
            full,
            pltpu.SMEM(pairs.shape, jnp.int32),
            pltpu.SMEM(tile_counts.shape, jnp.int32),
            pltpu.VMEM(src_rows, jnp.float32),
            pltpu.VMEM(tgt_rows, jnp.float32),
        ),
        in_specs=[hbm] * 4,
        out_specs=(vmem, vmem, smem, smem, vmem, vmem),
        scratch_shapes=[
            pltpu.VMEM(tile_cost.shape, tile_cost.dtype),
            pltpu.VMEM(src_rows, jnp.float32),
            pltpu.SemaphoreType.DMA((3,)),
            pltpu.SemaphoreType.DMA((slots,)),
        ],
        compiler_params=limit(10),
    )(*[pltpu.with_memory_space_constraint(array, pltpu.HBM) for array in inputs])
    row_parts = over_torus(row_part, "tgt", log_sum)
    col_part, plan, tops = over_tiles(
        first_columns, (scores, row_parts, src_mass), (by_tgt, full, tall), [src_rows, tgt_rows]
    )
    col_parts = over_torus(col_part, "src", log_sum)
    row_part, scale = over_tiles(
        later_rows, (plan, tops, col_parts, tgt_mass), (by_src, tall), [tgt_rows, src_rows]
    )
    row_parts = over_torus(row_part, "tgt", sum)
    col_part, rows = over_tiles(
        later_columns,
        (plan, scale, row_parts, src_mass),
        (by_tgt, jax.ShapeDtypeStruct(src_rows, jnp.float32)),
        [tgt_rows],
    )
    col_parts = over_torus(col_part, "src", sum)
    share = src_mass.size // group
    half = group // 2
    wire = jax.ShapeDtypeStruct((half, dim + 8, share), jnp.bfloat16)
    mine, other = over_tiles(
        map_tiles,
        (plan, scale, rows, col_parts, tgt_mass, targets_t),
        (jax.ShapeDtypeStruct((half, dim + 8, share), jnp.float32), wire),
        [tgt_rows, (dim, src_mass.size), src_rows],
        16,
        [pltpu.VMEM((edge, edge), jnp.bfloat16)] * 2,
    )
    (got,) = exchange(other, "tgt", (1,))
    block = jax.ShapeDtypeStruct((1, *wire.shape[1:]), wire.dtype)
    joined = pl.pallas_call(
        functools.partial(join_pair, dim, "tgt"),
        out_shape=[block] * half,
        in_specs=[vmem] * 2,
        out_specs=[vmem] * half,
        compiler_params=small,
    )(mine, got)
    order = sorted(range(1, half), key=lambda k: -min(k, half - k))
    parts = [joined[0], *[ahead(joined[k], "tgt", k) for k in order]]
    return pl.pallas_call(
        functools.partial(finish, dim),
        out_shape=jax.ShapeDtypeStruct((dim, share), jnp.float32),
        in_specs=[vmem] * half,
        out_specs=vmem,
        compiler_params=small,
    )(*parts)


def solution(mesh):
    return jax.shard_map(
        local,
        mesh=mesh,
        in_specs=(
            P(("src", "tgt"), None, None),
            P(("src", "tgt"), None),
            P(("src", "tgt")),
            P("src"),
            P("tgt"),
            P(None, "tgt"),
        ),
        out_specs=P(None, ("src", "tgt")),
        check_vma=False,
    )
```
